128 devices in a mesh: gx: 4 (over x_lo, core), gy: 4 (over y), gz: 8 (over x_hi, z).
Axes of the slice: x: 4 (x_hi: 2, x_lo: 2; x = x_hi * 2 + x_lo), y: 4, z: 4, core: 2. Of those that a mesh axis runs over, the one named last changes fastest.
Arguments:
- positions: float32 [8, 4, 16, 3, 128], P('gx', 'gy', 'gz'), may hold values from 0 to 1
- features: bfloat16 [8, 4, 16, 128, 128], P('gx', 'gy', 'gz'), may hold values from -6 to 6
- cell_count: int32 [8, 4, 16], P('gx', 'gy', 'gz'), may hold values from 64 to 128
- pair_mask: int32 [27, 8, 4, 16], P(None, 'gx', 'gy', 'gz'), may hold values from 0 to 1, as said below
- scalar_radial: float32 [4, 128], replicated, may hold values from -2 to 2
- vector_radial: float32 [4, 128], replicated, may hold values from -2 to 2
- mix_weight: bfloat16 [128, 128], replicated, may hold values from -0.5 to 0.5
- out_weight: float32 [128], replicated, may hold values from -0.5 to 0.5
Outputs:
- atom_energy: float32 [8, 4, 16, 128], P('gx', 'gy', 'gz')
- forces: float32 [8, 4, 16, 3, 128], P('gx', 'gy', 'gz')
The draws below stay inside these ranges and needn't reach their ends.
Inputs may be any that keep to these rules, and one draw needn't show every extreme that they name: pair_mask[o, c] equals pair_mask[26 - o, c + s_o] with periodic wrap, and pair_mask[13] is all ones.
All inputs are finite; a program needn't handle non-finite values.
Results may differ from the reference program's by a relative error of at most 0.0054.
Values may be sent and summed in bfloat16 or wider, within the bound.
No kernel may reach another device: no remote copies, remote signals or barrier semaphores. Data moves between devices by JAX's collectives and lax.ppermute only.
A program may use at most 128 MiB of HBM per device.

```python
import jax
import jax.numpy as jnp
from jax import lax

ATOMS = 128
CH = 128
NB = 4
CX = 2
CY = 1
CZ = 2
NXC = 8
NYC = 4
NZC = 16


def draw_pair_mask(key, part):
    key_level, key_bits = jax.random.split(jax.random.fold_in(key, 17))
    level = jax.random.randint(key_level, (NXC, NYC, NZC), 15, 90)
    votes = jax.random.randint(key_bits, (27, NXC, NYC, NZC), 0, 100)
    raw = (votes < level[None]).astype(jnp.int32)
    rows = []
    for offset_index in range(27):
        step_x = offset_index // 9 - 1
        step_y = offset_index // 3 % 3 - 1
        step_z = offset_index % 3 - 1
        partner = jnp.roll(raw[26 - offset_index], (-step_x, -step_y, -step_z), axis=(0, 1, 2))
        rows.append(jnp.maximum(raw[offset_index], partner))
    return jnp.stack(rows).at[13].set(1)


def set_ends(array, rng, least, largest):
    extent = array.shape
    place = [jax.random.randint(jax.random.fold_in(rng, axis), (), 0, extent[axis]) for axis in range(len(extent))]
    array = array.at[tuple(place)].set(least)
    longest = extent.index(max(extent))
    place[longest] = (place[longest] + 1) % extent[longest]
    return array.at[tuple(place)].set(largest)


def steps_of(rng, dims, shards, low, high):
    gain, own = 1.0, jax.random.fold_in(rng, 6)
    for dim, shards_of in shards:
        heights = jnp.exp(jax.random.uniform(jax.random.fold_in(own, dim), (shards_of,), jnp.float32, low / len(shards), high / len(shards)))
        gain = gain * jnp.repeat(heights, dims[dim] // shards_of).reshape([-1 if axis == dim else 1 for axis in range(len(dims))])
    return gain


def bell_draw(key, extent, deviation, reach, cuts=(), held_as=jnp.bfloat16):
    gain = steps_of(key, extent, cuts, -0.22, 0.18) if cuts else 1.0
    array = jax.random.normal(key, extent, jnp.float32) * deviation * gain
    return jnp.minimum(jnp.maximum(array, -reach), reach).astype(held_as)


def setup_inputs(seed: int = 0) -> dict:
    streams_of = jax.random.split(jax.random.key(seed), 9)
    positions = jnp.clip(1.0 * jax.random.uniform(streams_of[0], (NXC, NYC, NZC, 3, ATOMS), jnp.float32) ** steps_of(streams_of[0], (NXC, NYC, NZC, 3, ATOMS), ((0, 4), (1, 4), (2, 8)), -0.2, 0.2), 0.0, 1.0)
    features = bell_draw(streams_of[1], (NXC, NYC, NZC, CH, ATOMS), 1.0, 6.0, ((0, 4), (1, 4), (2, 8)))
    cell_count = set_ends(jax.random.randint(streams_of[2], (NXC, NYC, NZC), ATOMS // 2, ATOMS + 1), jax.random.fold_in(streams_of[2], 1), ATOMS // 2, ATOMS).astype(jnp.int32)
    pair_mask = draw_pair_mask(jax.random.fold_in(streams_of[8], 71), 0)
    scalar_radial = bell_draw(streams_of[4], (NB, CH), 0.15, 2.0, (), jnp.float32)
    vector_radial = bell_draw(streams_of[5], (NB, CH), 0.15, 2.0, (), jnp.float32)
    mix_weight = bell_draw(streams_of[6], (CH, CH), CH ** -0.5, 0.5)
    out_weight = bell_draw(streams_of[7], (CH,), CH ** -0.5, 0.5, (), jnp.float32)
    return dict(positions=positions, features=features, cell_count=cell_count, pair_mask=pair_mask, scalar_radial=scalar_radial, vector_radial=vector_radial, mix_weight=mix_weight, out_weight=out_weight)


PI_VALUE = 3.141592653589793
HIGHEST = lax.Precision.HIGHEST

def rounded(values):
    return lax.optimization_barrier(values.astype(jnp.bfloat16)).astype(jnp.float32)

def offset_vector(offset_index):
    return jnp.stack([offset_index // 9 - 1, offset_index // 3 % 3 - 1, offset_index % 3 - 1]).astype(jnp.int32)

def geometry(own_position, far_position, own_living, far_living, kept_tiles, displace, self_tile):
    displacement = far_position[:, :, None, :] + displace[None, :, None, None] - own_position[:, :, :, None]
    squared = lax.optimization_barrier(jnp.sum(displacement * displacement, axis=1))
    identity = jnp.eye(own_position.shape[2], dtype=jnp.float32)
    pair_weight = own_living[:, :, None] * far_living[:, None, :] * kept_tiles[:, None, None] * (1.0 - self_tile * identity)[None]
    pair_weight = jnp.where(squared < 1.0, pair_weight, 0.0)
    inside = pair_weight > 0.5
    radius = jnp.sqrt(jnp.where(inside, squared, 1.0))
    envelope = jnp.where(inside, (1.0 - squared) ** 2, 0.0)
    orders = jnp.arange(NB).astype(jnp.float32)
    radial_basis = envelope[:, None] * jnp.cos(PI_VALUE * orders[None, :, None, None] * radius[:, None])
    direction = displacement / radius[:, None]
    vector = radial_basis[:, :, None] * direction[:, None]
    return (radial_basis, vector)

def pair_messages(radial_basis, vector, far_scalar, far_vector):
    scalar_part = jnp.einsum('nkij,nkcj->nci', rounded(radial_basis), far_scalar.astype(jnp.float32), precision=HIGHEST)
    vector_part = jnp.einsum('nkaij,nkcj->naci', rounded(vector), far_vector.astype(jnp.float32), precision=HIGHEST)
    return jnp.concatenate([scalar_part[:, None], vector_part], axis=1)

def node_update(features, messages, living, mix_weight, out_weight):
    mixed_in = features.astype(jnp.float32) + messages[:, 0] + lax.optimization_barrier(jnp.sum(messages[:, 1:] ** 2, axis=1))
    mixing = mix_weight.astype(jnp.float32)
    hidden = jnp.einsum('nci,cd->ndi', rounded(mixed_in), mixing, precision=HIGHEST)
    sigmoid = jax.nn.sigmoid(hidden)
    energy = lax.optimization_barrier(jnp.sum(out_weight[None, :, None] * hidden * sigmoid, axis=1)) * living
    derivative = sigmoid * (1.0 + hidden * (1.0 - sigmoid))
    tangent = rounded(out_weight[None, :, None] * derivative * living[:, None, :])
    gradient = jnp.einsum('ndi,cd->nci', tangent, mixing, precision=HIGHEST)
    scalar_grad = gradient.astype(jnp.bfloat16)
    vector_grad = (2.0 * messages[:, 1:] * gradient[:, None]).astype(jnp.bfloat16)
    return (energy, jnp.concatenate([scalar_grad[:, None], vector_grad], axis=1))

def sensitivities(own_grad, far_grad, own_scalar, far_scalar, own_vector, far_vector):
    og = own_grad.astype(jnp.float32)
    fg = far_grad.astype(jnp.float32)
    pull = jnp.einsum('nci,nkcj->nkij', og[:, 0], far_scalar.astype(jnp.float32), precision=HIGHEST)
    pull = pull + jnp.einsum('ncj,nkci->nkij', fg[:, 0], own_scalar.astype(jnp.float32), precision=HIGHEST)
    turn = jnp.einsum('naci,nkcj->nkaij', og[:, 1:], far_vector.astype(jnp.float32), precision=HIGHEST)
    turn = turn - jnp.einsum('nacj,nkci->nkaij', fg[:, 1:], own_vector.astype(jnp.float32), precision=HIGHEST)
    return (pull, turn)

def reference(positions, features, cell_count, pair_mask, scalar_radial, vector_radial, mix_weight, out_weight):
    slots = jnp.arange(ATOMS, dtype=jnp.int32)
    living = (slots[None, None, None, :] < cell_count[..., None]).astype(jnp.float32)
    feature_wide = features.astype(jnp.float32)
    scalar_table = (scalar_radial[None, None, None, :, :, None] * feature_wide[:, :, :, None]).astype(jnp.bfloat16)
    vector_table = (vector_radial[None, None, None, :, :, None] * feature_wide[:, :, :, None]).astype(jnp.bfloat16)
    kept_all = pair_mask.astype(jnp.float32)
    group = CX * CY * CZ
    blocks = NXC * NYC * NZC // group

    def blocked(values):
        return values.reshape((blocks, group) + values.shape[3:])

    def rolled(values, offset_step):
        return jnp.roll(values, (-offset_step[0], -offset_step[1], -offset_step[2]), axis=(0, 1, 2))

    def message_turn(summed, offset_index):
        offset_step = offset_vector(offset_index)
        displace = offset_step.astype(jnp.float32)
        self_tile = (offset_index == 13).astype(jnp.float32)
        kept = lax.dynamic_index_in_dim(kept_all, offset_index, 0, keepdims=False)

        def one_block(items):
            own_pos, own_liv, kept_block, far_pos, far_liv, far_sca, far_vec = items
            radial_basis, vector = geometry(own_pos, far_pos, own_liv, far_liv, kept_block, displace, self_tile)
            return pair_messages(radial_basis, vector, far_sca, far_vec)
        result = lax.map(one_block, (blocked(positions), blocked(living), blocked(kept), blocked(rolled(positions, offset_step)), blocked(rolled(living, offset_step)), blocked(rolled(scalar_table, offset_step)), blocked(rolled(vector_table, offset_step))))
        return (summed + result, None)
    start_messages = jnp.zeros((blocks, group, 4, CH, ATOMS), jnp.float32)
    messages, _ = lax.scan(message_turn, start_messages, jnp.arange(27, dtype=jnp.int32))
    total_cells = NXC * NYC * NZC
    energy, node_grad = node_update(features.reshape(total_cells, CH, ATOMS), messages.reshape(total_cells, 4, CH, ATOMS), living.reshape(total_cells, ATOMS), mix_weight, out_weight)
    node_grad = node_grad.reshape(NXC, NYC, NZC, 4, CH, ATOMS)

    def force_turn(summed, offset_index):
        offset_step = offset_vector(offset_index)
        displace = offset_step.astype(jnp.float32)
        self_tile = (offset_index == 13).astype(jnp.float32)
        kept = lax.dynamic_index_in_dim(kept_all, offset_index, 0, keepdims=False)

        def one_block(items):
            own_pos, own_liv, kept_block, own_gr, own_sca, own_vec, far_pos, far_liv, far_gr, far_sca, far_vec = items
            pull, turn = sensitivities(own_gr, far_gr, own_sca, far_sca, own_vec, far_vec)

            def local_geometry(moved):
                return geometry(moved, far_pos, own_liv, far_liv, kept_block, displace, self_tile)
            _, pullback = jax.vjp(local_geometry, own_pos)
            return -pullback((pull, turn))[0]
        result = lax.map(one_block, (blocked(positions), blocked(living), blocked(kept), blocked(node_grad), blocked(scalar_table), blocked(vector_table), blocked(rolled(positions, offset_step)), blocked(rolled(living, offset_step)), blocked(rolled(node_grad, offset_step)), blocked(rolled(scalar_table, offset_step)), blocked(rolled(vector_table, offset_step))))
        return (summed + result, None)
    start_forces = jnp.zeros((blocks, group, 3, ATOMS), jnp.float32)
    forces, _ = lax.scan(force_turn, start_forces, jnp.arange(27, dtype=jnp.int32))
    return (energy.reshape(NXC, NYC, NZC, ATOMS), forces.reshape(NXC, NYC, NZC, 3, ATOMS))
```

```python
import functools

import jax
import jax.numpy as jnp
from jax import lax
from jax.experimental import pallas as pl
from jax.experimental.pallas import tpu as pltpu
from jax.sharding import PartitionSpec as P

NB = 4
AWAY = 1024.0
COS = (
    0.9999992107823212,
    -4.934745088941006,
    4.058041088814663,
    -1.3323690864736755,
    0.22965035984452822,
    -0.02057725158958951,
)
DCOS = (
    -4.934801893702061,
    8.117402063821372,
    -4.005527851534531,
    0.940201031496376,
    -0.12683837449652113,
    0.009565323992306946,
)
ROWS = 16


def horner(coefs, q):
    total = q * coefs[-1] + coefs[-2]
    for coef in coefs[-3::-1]:
        total = total * q + coef
    return total


def orders(x):
    x2 = x + x
    c2 = x2 * x - 1.0
    return None, x, c2, x2 * c2 - x


def lanes_to_sublanes(row):
    n = row.shape[-1]
    return jnp.broadcast_to(row, (n, n)).T


def kernel(
    dims,
    kept_ref,
    count_ref,
    before_ref,
    mid_ref,
    after_ref,
    pos_ref,
    radial_ref,
    mix_ref,
    mix_t_ref,
    out_weight_ref,
    energy_ref,
    force_ref,
    react_ref,
    tiles_ref,
    rad_col_ref,
    s_ref,
    v_ref,
    st_ref,
    vt_ref,
    own_ref,
    diag_ref,
    geo_ref,
    lhs_b_ref,
    lhs_v_ref,
    acc_ref,
    grad_ref,
    pull_ref,
    turn_ref,
    row_force_ref,
    col_ref,
):
    cells_x, cells_y, cells_z = dims
    ny, nz = cells_y + 2, cells_z + 2
    plane = ny * nz
    n = 128

    for m in range(2 * NB):
        rad_col_ref[m] = lanes_to_sublanes(radial_ref[m : m + 1, :])

    def tables(src_ref, base, cell):
        f = src_ref[cell].astype(jnp.float32)
        ft = f.T
        e = base + cell
        for m in range(NB):
            at = pl.ds(m * n, n)
            s_ref[e, :, at] = (rad_col_ref[m] * f).astype(jnp.bfloat16)
            v_ref[e, :, at] = (rad_col_ref[NB + m] * f).astype(jnp.bfloat16)
            st_ref[e, at, :] = (radial_ref[m : m + 1, :] * ft).astype(jnp.bfloat16)
            vt_ref[e, at, :] = (radial_ref[NB + m : NB + m + 1, :] * ft).astype(jnp.bfloat16)

    for src_ref, base, planes in (
        (before_ref, 0, 1),
        (mid_ref, plane, cells_x),
        (after_ref, plane * (cells_x + 1), 1),
    ):

        def table_step(cell, carry, src_ref=src_ref, base=base):
            tables(src_ref, base, cell)
            return carry

        lax.fori_loop(0, planes * plane, table_step, 0)

    diag_ref[0] = jnp.zeros((n, n), jnp.float32)
    diag_ref[1] = (
        lax.broadcasted_iota(jnp.int32, (n, n), 0) == lax.broadcasted_iota(jnp.int32, (n, n), 1)
    ).astype(jnp.float32)
    col_ref[...] = jnp.zeros_like(col_ref)

    def one_cell(cell, carry):
        ix = cell // (cells_y * cells_z)
        iy = cell // cells_z % cells_y
        iz = cell % cells_z
        home = (ix + 1) * plane + (iy + 1) * nz + iz + 1
        count = count_ref[cell]

        def listing(o, length):
            tiles_ref[length] = o
            return length + kept_ref[o, cell]

        length = lax.fori_loop(0, 27, listing, 0)

        alive_row = lax.broadcasted_iota(jnp.int32, (1, n), 1) < count
        for a in range(3):
            row = pos_ref[home, a : a + 1, :]
            own_ref[a] = lanes_to_sublanes(jnp.where(alive_row, row, -AWAY))

        def place(index):
            o = tiles_ref[index]
            sx, sy, sz = o // 9 - 1, o // 3 % 3 - 1, o % 3 - 1
            far = home + sx * plane + sy * nz + sz
            rows = [
                pos_ref[far, a : a + 1, :] + step.astype(jnp.float32)
                for a, step in enumerate((sx, sy, sz))
            ]
            return o, far, rows

        acc_ref[...] = jnp.zeros_like(acc_ref)

        def forward(index, carry):
            o, far, rows = place(index)
            self_tile = (o == 13).astype(jnp.int32)
            for r in range(0, n, ROWS):
                at = pl.ds(r, ROWS)
                d = [rows[a] - own_ref[a, at, :] for a in range(3)]
                q = d[0] * d[0] + d[1] * d[1] + d[2] * d[2]
                q = jnp.minimum(jnp.maximum(q, diag_ref[self_tile, at, :]), 1.0)
                t = 1.0 - q
                u = t * t
                x = horner(COS, q)
                inverse = lax.rsqrt(q)
                geo_ref[index, 0, at, :] = q
                geo_ref[index, 1, at, :] = x
                geo_ref[index, 2, at, :] = inverse
                waves = orders(x)
                for m in range(NB):
                    lanes = pl.ds(m * n, n)
                    b = u * waves[m] if m else u
                    w = b * inverse
                    lhs_b_ref[at, lanes] = b.astype(jnp.bfloat16)
                    for a in range(3):
                        lhs_v_ref[pl.ds(a * n + r, ROWS), lanes] = (w * d[a]).astype(jnp.bfloat16)
            acc_ref[0:n, :] += jnp.dot(
                lhs_b_ref[...], st_ref[far], preferred_element_type=jnp.float32
            )
            acc_ref[n:, :] += jnp.dot(
                lhs_v_ref[...], vt_ref[far], preferred_element_type=jnp.float32
            )
            return carry

        lax.fori_loop(0, length, forward, 0)

        m0 = acc_ref[0:n, :]
        ma = [acc_ref[(a + 1) * n : (a + 2) * n, :] for a in range(3)]
        own_feature = mid_ref[home - plane].astype(jnp.float32).T
        z = own_feature + m0 + (ma[0] * ma[0] + ma[1] * ma[1] + ma[2] * ma[2])
        hidden = jnp.dot(
            z.astype(jnp.bfloat16), mix_ref[...], preferred_element_type=jnp.float32
        )
        sigmoid = 1.0 / (1.0 + jnp.exp(-hidden))
        weight = out_weight_ref[...]
        per = (weight * hidden * sigmoid).T
        energy_ref[pl.ds(cell, 1), :] = jnp.where(
            alive_row, jnp.sum(per, axis=0, keepdims=True), 0.0
        )
        alive = lax.broadcasted_iota(jnp.int32, (n, n), 0) < count
        derivative = sigmoid * (1.0 + hidden * (1.0 - sigmoid))
        tangent = jnp.where(alive, weight * derivative, 0.0).astype(jnp.bfloat16)
        g = jnp.dot(tangent, mix_t_ref[...], preferred_element_type=jnp.float32)
        grad_ref[0:n, :] = g.astype(jnp.bfloat16)
        for a in range(3):
            grad_ref[(a + 1) * n : (a + 2) * n, :] = (2.0 * ma[a] * g).astype(jnp.bfloat16)

        row_force_ref[...] = jnp.zeros_like(row_force_ref)

        def backward(index, carry):
            o, far, rows = place(index)
            pull_ref[...] = jnp.dot(
                grad_ref[0:n, :], s_ref[far], preferred_element_type=jnp.float32
            )
            turn_ref[...] = jnp.dot(
                grad_ref[n:, :], v_ref[far], preferred_element_type=jnp.float32
            )
            col = [jnp.zeros((8, n), jnp.float32) for _ in range(3)]
            for r in range(0, n, 8):
                at = pl.ds(r, 8)
                d = [rows[a] - own_ref[a, at, :] for a in range(3)]
                q = geo_ref[index, 0, at, :]
                x = geo_ref[index, 1, at, :]
                inverse = geo_ref[index, 2, at, :]
                t = 1.0 - q
                u = t * t
                dx = horner(DCOS, q)
                turns = [
                    [turn_ref[pl.ds(a * n + r, 8), pl.ds(m * n, n)] for m in range(NB)]
                    for a in range(3)
                ]
                tau = [
                    turns[0][m] * d[0] + turns[1][m] * d[1] + turns[2][m] * d[2]
                    for m in range(NB)
                ]
                mix = [pull_ref[at, pl.ds(m * n, n)] + inverse * tau[m] for m in range(NB)]

                _, _, c2, c3 = orders(x)

                def series(values):
                    return (values[0] + x * values[1]) + (c2 * values[2] + c3 * values[3])

                e1 = series(mix)
                e2 = mix[1] + (4.0 * x) * mix[2] + (6.0 * c2 + 3.0) * mix[3]
                e3 = series(tau)
                ui = u * inverse
                along = (-4.0 * t) * e1 + ((u + u) * dx) * e2 - (ui * (inverse * inverse)) * e3
                for a in range(3):
                    f = d[a] * along + ui * series(turns[a])
                    row_force_ref[a, at, :] += f
                    col[a] = col[a] + f
            for a in range(3):
                col_ref[far, a] += col[a]
            return carry

        lax.fori_loop(0, length, backward, 0)
        for a in range(3):
            force_ref[cell, a : a + 1, :] = jnp.sum(
                row_force_ref[a].T, axis=0, keepdims=True
            )
        return carry

    lax.fori_loop(0, cells_x * cells_y * cells_z, one_cell, 0)

    def reduce(e, carry):
        react_ref[e] = jnp.sum(col_ref[e], axis=1)
        return carry

    lax.fori_loop(0, plane * (cells_x + 2), reduce, 0)


def local(dims, kept, count, before, mid, after, pos, radial, mix, out_weight):
    cells_x, cells_y, cells_z = dims
    cells = cells_x * cells_y * cells_z
    wide = (cells_x + 2) * (cells_y + 2) * (cells_z + 2)
    n = 128
    vmem = pl.BlockSpec(memory_space=pltpu.VMEM)
    smem = pl.BlockSpec(memory_space=pltpu.SMEM)
    f32, bf16 = jnp.float32, jnp.bfloat16
    return pl.pallas_call(
        functools.partial(kernel, dims),
        out_shape=(
            jax.ShapeDtypeStruct((cells, n), f32),
            jax.ShapeDtypeStruct((cells, 3, n), f32),
            jax.ShapeDtypeStruct((wide, 3, n), f32),
        ),
        in_specs=[smem, smem] + [vmem] * 8,
        out_specs=(vmem, vmem, vmem),
        scratch_shapes=[
            pltpu.SMEM((32,), jnp.int32),
            pltpu.VMEM((2 * NB, n, n), f32),
            pltpu.VMEM((wide, n, NB * n), bf16),
            pltpu.VMEM((wide, n, NB * n), bf16),
            pltpu.VMEM((wide, NB * n, n), bf16),
            pltpu.VMEM((wide, NB * n, n), bf16),
            pltpu.VMEM((3, n, n), f32),
            pltpu.VMEM((2, n, n), f32),
            pltpu.VMEM((27, 3, n, n), f32),
            pltpu.VMEM((n, NB * n), bf16),
            pltpu.VMEM((3 * n, NB * n), bf16),
            pltpu.VMEM((4 * n, n), f32),
            pltpu.VMEM((4 * n, n), bf16),
            pltpu.VMEM((n, NB * n), f32),
            pltpu.VMEM((3 * n, NB * n), f32),
            pltpu.VMEM((3, n, n), f32),
            pltpu.VMEM((wide, 3, 8, n), f32),
        ],
        compiler_params=pltpu.CompilerParams(vmem_limit_bytes=60 * 1024 * 1024),
        name="pair_kernel",
    )(kept, count, before, mid, after, pos, radial, mix, mix.T, out_weight.reshape(1, n))


def swap(axis, up_value, down_value):
    devices = lax.axis_size(axis)
    up = [(i, (i + 1) % devices) for i in range(devices)]
    down = [(j, i) for i, j in up]
    return lax.ppermute(up_value, axis, up), lax.ppermute(down_value, axis, down)


def widened(shard, axis, dim):
    length = shard.shape[dim]
    last = lax.slice_in_dim(shard, length - 1, length, axis=dim)
    leading = lax.slice_in_dim(shard, 0, 1, axis=dim)
    return swap(axis, last, leading)


def returned(wide, axis, dim):
    length = wide.shape[dim]
    high = lax.slice_in_dim(wide, length - 1, length, axis=dim)
    low = lax.slice_in_dim(wide, 0, 1, axis=dim)
    from_below, from_above = swap(axis, high, low)
    core = lax.slice_in_dim(wide, 1, length - 1, axis=dim)
    rest = length - 3

    def pad(piece, lo, hi):
        widths = [(0, 0)] * wide.ndim
        widths[dim] = (lo, hi)
        return jnp.pad(piece, widths)

    return core + pad(from_below, 0, rest) + pad(from_above, rest, 0)


def shards(
    positions, features, cell_count, pair_mask, scalar_radial, vector_radial, mix_weight, out_weight
):
    cells_x, cells_y, cells_z, _, n = positions.shape
    dims = (cells_x, cells_y, cells_z)
    cells = cells_x * cells_y * cells_z
    slots = jnp.arange(n, dtype=jnp.int32)
    living = slots[None, None, None, None, :] < cell_count[..., None, None]
    placed = jnp.where(living, positions, AWAY)
    wide_feature = features
    for axis, dim in (("gz", 2), ("gy", 1)):
        below, above = widened(placed, axis, dim)
        placed = jnp.concatenate([below, placed, above], axis=dim)
        below, above = widened(wide_feature, axis, dim)
        wide_feature = jnp.concatenate([below, wide_feature, above], axis=dim)
    below, above = widened(placed, "gx", 0)
    placed = jnp.concatenate([below, placed, above], axis=0)
    before, after = widened(wide_feature, "gx", 0)
    flat = lambda v: v.reshape((-1,) + v.shape[3:])
    radial = jnp.concatenate([scalar_radial, vector_radial], axis=0)
    energy, force, react = local(
        dims,
        pair_mask.reshape(27, cells),
        cell_count.reshape(cells),
        flat(before),
        flat(wide_feature),
        flat(after),
        flat(placed),
        radial,
        mix_weight,
        out_weight,
    )
    react = react.reshape(cells_x + 2, cells_y + 2, cells_z + 2, 3, n)
    for axis, dim in (("gx", 0), ("gy", 1), ("gz", 2)):
        react = returned(react, axis, dim)
    return (
        energy.reshape(cells_x, cells_y, cells_z, n),
        force.reshape(cells_x, cells_y, cells_z, 3, n) - react,
    )


def solution(mesh):
    return jax.shard_map(
        shards,
        mesh=mesh,
        in_specs=(
            P("gx", "gy", "gz", None, None),
            P("gx", "gy", "gz", None, None),
            P("gx", "gy", "gz"),
            P(None, "gx", "gy", "gz"),
            P(),
            P(),
            P(),
            P(),
        ),
        out_specs=(P("gx", "gy", "gz", None), P("gx", "gy", "gz", None, None)),
        check_vma=False,
    )
```

```python
import functools

import jax
import jax.numpy as jnp
from jax import lax
from jax.experimental import pallas as pl
from jax.experimental.pallas import tpu as pltpu
from jax.sharding import PartitionSpec as P

NB = 4
AWAY = 1024.0
COS = (
    0.9999992107823212,
    -4.934745088941006,
    4.058041088814663,
    -1.3323690864736755,
    0.22965035984452822,
    -0.02057725158958951,
)
HALF_ROOT_PI = -(2.0**0.5) * 3.141592653589793
HEIGHT = 144
UNROLL = 4
LAG = 1
ROWS = 16
SHAPE_DEPTH = 8
FORCE_DEPTH = 4


def zeros_after(value):
    return jnp.minimum(jnp.abs(value[0:1, :]), 0.0)


def behind(rows, after):
    return rows if after is None else [row + after for row in rows]


def horner(coefs, q):
    total = q * coefs[-1] + coefs[-2]
    for coef in coefs[-3::-1]:
        total = total * q + coef
    return total


def orders(x):
    x2 = x + x
    c2 = x2 * x - 1.0
    return None, x, c2, x2 * c2 - x


def lanes_to_sublanes(row):
    n = row.shape[-1]
    return jnp.broadcast_to(row, (n, n)).T


def kernel(
    dims,
    mask_ref,
    held_ref,
    before_ref,
    mid_ref,
    after_ref,
    scalar_ref,
    vector_ref,
    mix_ref,
    out_weight_ref,
    energy_ref,
    force_ref,
    react_ref,
    tiles_ref,
    rad_col_ref,
    pos_ref,
    s_ref,
    v_ref,
    own_ref,
    diag_ref,
    geo_ref,
    lhs0_ref,
    lhs1_ref,
    acc_ref,
    grad_ref,
    pull0_ref,
    turn0_ref,
    pull1_ref,
    turn1_ref,
    row_force_ref,
    col_ref,
):
    cells_x, cells_y, cells_z = dims
    cells = cells_x * cells_y * cells_z
    ny, nz = cells_y + 2, cells_z + 2
    plane = ny * nz
    n = 128

    def home_of(cell):
        ix = cell // (cells_y * cells_z)
        iy = cell // cells_z % cells_y
        iz = cell % cells_z
        return (ix + 1) * plane + (iy + 1) * nz + iz + 1

    def count_of(cell):
        ix = cell // (cells_y * cells_z)
        return held_ref[ix, cell // cells_z % cells_y, cell % cells_z]

    length = jnp.int32(0)
    wide = plane * (cells_x + 2)
    for cell in range(cells):
        home = home_of(cell)
        at = (cell // (cells_y * cells_z), cell // cells_z % cells_y, cell % cells_z)
        for o in range(27):
            far = home + (o // 9 - 1) * plane + (o // 3 % 3 - 1) * nz + o % 3 - 1
            tiles_ref[length] = (((far * 64 + far) * 2 + int(o == 13)) * 8) + cell
            length = length + mask_ref[(o,) + at]
    for extra in range(UNROLL):
        tiles_ref[length + extra] = (wide * 64 + home_of(0)) * 16
    groups = (length + UNROLL - 1) // UNROLL

    for m in range(NB):
        rad_col_ref[m] = lanes_to_sublanes(scalar_ref[m : m + 1, :])
        rad_col_ref[NB + m] = lanes_to_sublanes(vector_ref[m : m + 1, :])

    def tables(src_ref, base, cell):
        f = src_ref[cell, 0:n, :].astype(jnp.float32)
        e = base + cell
        for m in range(NB):
            s_ref[e, m] = (rad_col_ref[m] * f).astype(jnp.bfloat16)
            v_ref[e, m] = (rad_col_ref[NB + m] * f).astype(jnp.bfloat16)
        parts = src_ref[cell, n:, :].astype(jnp.float32)
        at = (e // plane, e // nz % ny, e % nz)
        for a in range(3):
            row = parts[a : a + 1, :] + parts[3 + a : 4 + a, :] + parts[6 + a : 7 + a, :]
            pos_ref[e, a : a + 1, :] = row + at[a].astype(jnp.float32)

    for src_ref, base, planes in (
        (before_ref, 0, 1),
        (mid_ref, plane, cells_x),
        (after_ref, plane * (cells_x + 1), 1),
    ):

        def table_step(cell, carry, src_ref=src_ref, base=base):
            tables(src_ref, base, cell)
            return carry

        lax.fori_loop(0, planes * plane, table_step, 0, unroll=2)
    pos_ref[wide] = jnp.full((3, n), AWAY, jnp.float32)

    diag_ref[0] = jnp.zeros((n, n), jnp.float32)
    diag_ref[1] = (
        lax.broadcasted_iota(jnp.int32, (n, n), 0) == lax.broadcasted_iota(jnp.int32, (n, n), 1)
    ).astype(jnp.float32)
    col_ref[...] = jnp.zeros_like(col_ref)
    acc_ref[...] = jnp.zeros_like(acc_ref)
    row_force_ref[...] = jnp.zeros_like(row_force_ref)
    lhs1_ref[...] = jnp.zeros_like(lhs1_ref)

    lane = lax.broadcasted_iota(jnp.int32, (1, n), 1)

    def own_step(cell, carry):
        for a in range(3):
            row = pos_ref[home_of(cell), a : a + 1, :]
            own_ref[cell, a] = lanes_to_sublanes(jnp.where(lane < count_of(cell), row, -AWAY))
        return carry

    lax.fori_loop(0, cells, own_step, 0)

    def where_of(index):
        entry = tiles_ref[index]
        return entry & 7, (entry >> 3) & 1, (entry >> 4) & 63, entry >> 10

    def far_rows(place):
        return [pos_ref[place, a : a + 1, :] for a in range(3)]

    def wide_table(table_ref, far):
        return jnp.concatenate([table_ref[far, m] for m in range(NB)], axis=1)

    def shape_tile(index, lhs_ref, after):
        cell, self_tile, _, place = where_of(index)
        first_rows = far_rows(place)
        marks = [after] * SHAPE_DEPTH
        for r in range(0, n, ROWS):
            at = pl.ds(r, ROWS)
            rows = behind(first_rows, marks[-SHAPE_DEPTH])
            d = [rows[a] - own_ref[cell, a, at, :] for a in range(3)]
            q = d[0] * d[0] + d[1] * d[1] + d[2] * d[2]
            q = jnp.minimum(jnp.maximum(q, diag_ref[self_tile, at, :]), 1.0)
            t = 1.0 - q
            u = t * t
            x = horner(COS, q)
            inverse = lax.rsqrt(q)
            waves = orders(x)
            for k, kept in enumerate((t, x, inverse, waves[2], waves[3])):
                geo_ref[index, k, at, :] = kept
            for m in range(NB):
                b = u * waves[m] if m else u
                w = b * inverse
                lhs_ref[m, at, :] = b.astype(jnp.bfloat16)
                for a in range(3):
                    lhs_ref[m, pl.ds((a + 1) * n + r, ROWS), :] = (w * d[a]).astype(jnp.bfloat16)
            marks.append(zeros_after(w))
        return marks[-1]

    def gather_tile(index, lhs_ref):
        cell, _, far, _ = where_of(index)

        def contract(rows, table_ref):
            lhs = jnp.concatenate([lhs_ref[m, rows, :] for m in range(NB)], axis=1)
            return lax.dot_general(
                lhs,
                wide_table(table_ref, far),
                (((1,), (1,)), ((), ())),
                preferred_element_type=jnp.float32,
            )

        acc_ref[cell, 0:n, :] += contract(pl.ds(0, n), s_ref)
        last = contract(pl.ds(n, 3 * n), v_ref)
        acc_ref[cell, n:, :] += last
        return zeros_after(last[3 * n - 8 :, :])

    lhs_refs = (lhs0_ref, lhs1_ref)

    def forward(group, carry):
        first = UNROLL * group
        gathered = [None] * LAG + [gather_tile(jnp.maximum(first - 1, 0), lhs1_ref)]
        after = None
        for k in range(UNROLL):
            if gathered[k] is not None:
                after = gathered[k] if after is None else after + gathered[k]
            after = shape_tile(first + k, lhs_refs[k % 2], after)
            if k < UNROLL - 1:
                gathered.append(gather_tile(first + k, lhs_refs[k % 2]))
        return carry

    lax.fori_loop(0, groups, forward, 0)
    gather_tile(UNROLL * groups - 1, lhs1_ref)

    def update(cell, carry):
        m0 = acc_ref[cell, 0:n, :]
        ma = [acc_ref[cell, (a + 1) * n : (a + 2) * n, :] for a in range(3)]
        own_feature = mid_ref[home_of(cell) - plane, 0:n, :].astype(jnp.float32).T
        z = own_feature + m0 + (ma[0] * ma[0] + ma[1] * ma[1] + ma[2] * ma[2])
        hidden = jnp.dot(
            z.astype(jnp.bfloat16), mix_ref[...], preferred_element_type=jnp.float32
        )
        sigmoid = 1.0 / (1.0 + jnp.exp(-hidden))
        weight = out_weight_ref[...]
        count = count_of(cell)
        per = (weight * hidden * sigmoid).T
        energy_ref[pl.ds(cell, 1), :] = jnp.where(
            lane < count, jnp.sum(per, axis=0, keepdims=True), 0.0
        )
        alive = lax.broadcasted_iota(jnp.int32, (n, n), 0) < count
        derivative = sigmoid * (1.0 + hidden * (1.0 - sigmoid))
        tangent = jnp.where(alive, weight * derivative, 0.0).astype(jnp.bfloat16)
        g = lax.dot_general(
            tangent, mix_ref[...], (((1,), (1,)), ((), ())), preferred_element_type=jnp.float32
        )
        grad_ref[cell, 0:n, :] = g.astype(jnp.bfloat16)
        for a in range(3):
            grad_ref[cell, (a + 1) * n : (a + 2) * n, :] = (2.0 * ma[a] * g).astype(jnp.bfloat16)
        return carry

    lax.fori_loop(0, cells, update, 0)

    def sense_tile(index, pull_ref, turn_ref):
        cell, _, far, _ = where_of(index)

        pull_ref[...] = jnp.dot(
            grad_ref[cell, 0:n, :], wide_table(s_ref, far), preferred_element_type=jnp.float32
        )
        turn_ref[...] = jnp.dot(
            grad_ref[cell, n:, :], wide_table(v_ref, far), preferred_element_type=jnp.float32
        )

    def force_tile(index, pull_ref, turn_ref, after):
        cell, _, far, place = where_of(index)
        first_rows = far_rows(place)
        marks = [after] * FORCE_DEPTH
        col = [jnp.zeros((8, n), jnp.float32) for _ in range(3)]
        for r in range(0, n, 8):
            at = pl.ds(r, 8)
            rows = behind(first_rows, marks[-FORCE_DEPTH])
            d = [rows[a] - own_ref[cell, a, at, :] for a in range(3)]
            t, x, inverse, c2, c3 = [geo_ref[index, k, at, :] for k in range(5)]
            u = t * t
            s2, s3 = 4.0 * x, 6.0 * c2 + 3.0

            def value(v):
                return (v[0] + x * v[1]) + (c2 * v[2] + c3 * v[3])

            def slope(v):
                return v[1] + (s2 * v[2] + s3 * v[3])

            pulls = [pull_ref[at, pl.ds(m * n, n)] for m in range(NB)]
            e1, e2 = value(pulls), slope(pulls)
            values, slopes = [], []
            for a in range(3):
                turns = [turn_ref[pl.ds(a * n + r, 8), pl.ds(m * n, n)] for m in range(NB)]
                values.append(value(turns))
                slopes.append(slope(turns))
            e3 = d[0] * values[0] + d[1] * values[1] + d[2] * values[2]
            e4 = d[0] * slopes[0] + d[1] * slopes[1] + d[2] * slopes[2]
            ui = u * inverse
            sine2 = jnp.maximum(1.0 - c2, 1e-12)
            bend = (HALF_ROOT_PI * 0.5) * (sine2 * lax.rsqrt(sine2))
            along = (
                (-4.0 * t) * (e1 + inverse * e3)
                + (ui * bend) * (e2 + inverse * e4)
                - (ui * (inverse * inverse)) * e3
            )
            for a in range(3):
                f = d[a] * along + ui * values[a]
                row_force_ref[cell, a, at, :] += f
                col[a] = col[a] + f
            marks.append(zeros_after(col[0]))
        for a in range(3):
            col_ref[far, a] += col[a]
        return marks[-1]

    sense_refs = ((pull0_ref, turn0_ref), (pull1_ref, turn1_ref))

    def backward(group, carry):
        first = UNROLL * group
        after = None
        for k in range(UNROLL):
            sense_tile(jnp.minimum(first + k + 1, length), *sense_refs[(k + 1) % 2])
            after = force_tile(first + k, *sense_refs[k % 2], after)
        return carry

    sense_tile(0, *sense_refs[0])
    lax.fori_loop(0, groups, backward, 0)

    def finish(cell, carry):
        for a in range(3):
            force_ref[cell, a : a + 1, :] = jnp.sum(
                row_force_ref[cell, a].T, axis=0, keepdims=True
            )
        return carry

    lax.fori_loop(0, cells, finish, 0)

    def reduce(e, carry):
        react_ref[e] = jnp.sum(col_ref[e], axis=1)
        return carry

    lax.fori_loop(0, plane * (cells_x + 2), reduce, 0)


def local(dims, mask, held, before, mid, after, scalar, vector, mix, out_weight):
    cells_x, cells_y, cells_z = dims
    cells = cells_x * cells_y * cells_z
    wide = (cells_x + 2) * (cells_y + 2) * (cells_z + 2)
    n = 128
    vmem = pl.BlockSpec(memory_space=pltpu.VMEM)
    smem = pl.BlockSpec(memory_space=pltpu.SMEM)
    f32, bf16 = jnp.float32, jnp.bfloat16
    return pl.pallas_call(
        functools.partial(kernel, dims),
        out_shape=(
            jax.ShapeDtypeStruct((cells, n), f32),
            jax.ShapeDtypeStruct((cells, 3, n), f32),
            jax.ShapeDtypeStruct((wide, 3, n), f32),
        ),
        in_specs=[smem, smem] + [vmem] * 7,
        out_specs=(vmem, vmem, vmem),
        scratch_shapes=[
            pltpu.SMEM((27 * cells + UNROLL,), jnp.int32),
            pltpu.VMEM((2 * NB, n, n), f32),
            pltpu.VMEM((wide + 1, 3, n), f32),
            pltpu.VMEM((wide, NB, n, n), bf16),
            pltpu.VMEM((wide, NB, n, n), bf16),
            pltpu.VMEM((cells, 3, n, n), f32),
            pltpu.VMEM((2, n, n), f32),
            pltpu.VMEM((27 * cells + UNROLL, 5, n, n), f32),
            pltpu.VMEM((NB, 4 * n, n), bf16),
            pltpu.VMEM((NB, 4 * n, n), bf16),
            pltpu.VMEM((cells, 4 * n, n), f32),
            pltpu.VMEM((cells, 4 * n, n), bf16),
            pltpu.VMEM((n, NB * n), f32),
            pltpu.VMEM((3 * n, NB * n), f32),
            pltpu.VMEM((n, NB * n), f32),
            pltpu.VMEM((3 * n, NB * n), f32),
            pltpu.VMEM((cells, 3, n, n), f32),
            pltpu.VMEM((wide, 3, 8, n), f32),
        ],
        compiler_params=pltpu.CompilerParams(vmem_limit_bytes=61 * 1024 * 1024),
        name="pair_kernel",
    )(mask, held, before, mid, after, scalar, vector, mix, out_weight.reshape(1, n))


def swap(axis, up_value, down_value):
    devices = lax.axis_size(axis)
    up = [(i, (i + 1) % devices) for i in range(devices)]
    down = [(j, i) for i, j in up]
    return lax.ppermute(up_value, axis, up), lax.ppermute(down_value, axis, down)


def widened(shard, axis, dim):
    length = shard.shape[dim]
    last = lax.slice_in_dim(shard, length - 1, length, axis=dim)
    leading = lax.slice_in_dim(shard, 0, 1, axis=dim)
    return swap(axis, last, leading)


def returned(wide, axis, dim):
    length = wide.shape[dim]
    high = lax.slice_in_dim(wide, length - 1, length, axis=dim)
    low = lax.slice_in_dim(wide, 0, 1, axis=dim)
    from_below, from_above = swap(axis, high, low)
    core = lax.slice_in_dim(wide, 1, length - 1, axis=dim)
    rest = length - 3

    def pad(piece, lo, hi):
        widths = [(0, 0)] * wide.ndim
        widths[dim] = (lo, hi)
        return jnp.pad(piece, widths)

    return core + pad(from_below, 0, rest) + pad(from_above, rest, 0)


def packed(positions, features, cell_count):
    n = positions.shape[-1]
    slots = jnp.arange(n, dtype=jnp.int32)
    rest = jnp.where(slots < cell_count[..., None, None], positions, AWAY)
    parts = []
    for _ in range(3):
        part = lax.reduce_precision(rest, 8, 7)
        parts.append(part)
        rest = rest - part
    spare = HEIGHT - n - 9
    parts.append(jnp.zeros(rest.shape[:3] + (spare, n), rest.dtype))
    rows = jnp.concatenate(parts, axis=3).astype(jnp.bfloat16)
    return jnp.concatenate([features, rows], axis=3)


def shards(
    positions, features, cell_count, pair_mask, scalar_radial, vector_radial, mix_weight, out_weight
):
    cells_x, cells_y, cells_z, _, n = positions.shape
    block = packed(positions, features, cell_count)
    for axis, dim in (("gz", 2), ("gy", 1)):
        below, above = widened(block, axis, dim)
        block = jnp.concatenate([below, block, above], axis=dim)
    before, after = widened(block, "gx", 0)
    flat = lambda v: v.reshape((-1,) + v.shape[3:])
    energy, force, react = local(
        (cells_x, cells_y, cells_z),
        pair_mask,
        cell_count,
        flat(before),
        flat(block),
        flat(after),
        scalar_radial,
        vector_radial,
        mix_weight,
        out_weight,
    )
    react = react.reshape(cells_x + 2, cells_y + 2, cells_z + 2, 3, n)
    for axis, dim in (("gx", 0), ("gy", 1), ("gz", 2)):
        react = returned(react, axis, dim)
    return (
        energy.reshape(cells_x, cells_y, cells_z, n),
        force.reshape(cells_x, cells_y, cells_z, 3, n) - react,
    )


def solution(mesh):
    return jax.shard_map(
        shards,
        mesh=mesh,
        in_specs=(
            P("gx", "gy", "gz", None, None),
            P("gx", "gy", "gz", None, None),
            P("gx", "gy", "gz"),
            P(None, "gx", "gy", "gz"),
            P(),
            P(),
            P(),
            P(),
        ),
        out_specs=(P("gx", "gy", "gz", None), P("gx", "gy", "gz", None, None)),
        check_vma=False,
    )
```

```python
import functools

import jax
import jax.numpy as jnp
from jax import lax
from jax.experimental import pallas as pl
from jax.experimental.pallas import tpu as pltpu
from jax.sharding import PartitionSpec as P

NB = 4
AWAY = 1024.0
COS = (
    0.9999992107823212,
    -4.934745088941006,
    4.058041088814663,
    -1.3323690864736755,
    0.22965035984452822,
    -0.02057725158958951,
)
HALF_ROOT_PI = -(2.0**0.5) * 3.141592653589793
HEIGHT = 144
UNROLL = 4
LAG = 1
ROWS = 16
SHAPE_DEPTH = 8
FORCE_DEPTH = 3


def zeros_after(value):
    return jnp.minimum(jnp.abs(value[0:1, :]), 0.0)


def behind(rows, after):
    return rows if after is None else [row + after for row in rows]


def horner(coefs, q):
    total = q * coefs[-1] + coefs[-2]
    for coef in coefs[-3::-1]:
        total = total * q + coef
    return total


def orders(x):
    x2 = x + x
    c2 = x2 * x - 1.0
    return None, x, c2, x2 * c2 - x


def lanes_to_sublanes(row):
    n = row.shape[-1]
    return jnp.broadcast_to(row, (n, n)).T


def kernel(
    dims,
    mask_ref,
    held_ref,
    before_ref,
    mid_ref,
    after_ref,
    scalar_ref,
    vector_ref,
    mix_ref,
    out_weight_ref,
    energy_ref,
    force_ref,
    react_ref,
    tiles_ref,
    rad_col_ref,
    pos_ref,
    s_ref,
    v_ref,
    own_ref,
    diag_ref,
    geo_ref,
    lhs0_ref,
    lhs1_ref,
    acc_ref,
    grad_ref,
    pull0_ref,
    turn0_ref,
    pull1_ref,
    turn1_ref,
    row_force_ref,
    col_ref,
):
    cells_x, cells_y, cells_z = dims
    cells = cells_x * cells_y * cells_z
    ny, nz = cells_y + 2, cells_z + 2
    plane = ny * nz
    n = 128

    def home_of(cell):
        ix = cell // (cells_y * cells_z)
        iy = cell // cells_z % cells_y
        iz = cell % cells_z
        return (ix + 1) * plane + (iy + 1) * nz + iz + 1

    def count_of(cell):
        ix = cell // (cells_y * cells_z)
        return held_ref[ix, cell // cells_z % cells_y, cell % cells_z]

    length = jnp.int32(0)
    wide = plane * (cells_x + 2)
    for cell in range(cells):
        home = home_of(cell)
        at = (cell // (cells_y * cells_z), cell // cells_z % cells_y, cell % cells_z)
        for o in range(27):
            far = home + (o // 9 - 1) * plane + (o // 3 % 3 - 1) * nz + o % 3 - 1
            tiles_ref[length] = (((far * 64 + far) * 2 + int(o == 13)) * 8) + cell
            length = length + mask_ref[(o,) + at]
    for extra in range(UNROLL):
        tiles_ref[length + extra] = (wide * 64 + home_of(0)) * 16
    groups = (length + UNROLL - 1) // UNROLL

    for m in range(NB):
        rad_col_ref[m] = lanes_to_sublanes(scalar_ref[m : m + 1, :])
        rad_col_ref[NB + m] = lanes_to_sublanes(vector_ref[m : m + 1, :])

    def tables(src_ref, base, cell):
        f = src_ref[cell, 0:n, :].astype(jnp.float32)
        e = base + cell
        for m in range(NB):
            s_ref[e, m] = (rad_col_ref[m] * f).astype(jnp.bfloat16)
            v_ref[e, m] = (rad_col_ref[NB + m] * f).astype(jnp.bfloat16)
        parts = src_ref[cell, n:, :].astype(jnp.float32)
        at = (e // plane, e // nz % ny, e % nz)
        for a in range(3):
            row = parts[a : a + 1, :] + parts[3 + a : 4 + a, :] + parts[6 + a : 7 + a, :]
            pos_ref[e, a : a + 1, :] = row + at[a].astype(jnp.float32)

    for src_ref, base, planes in (
        (before_ref, 0, 1),
        (mid_ref, plane, cells_x),
        (after_ref, plane * (cells_x + 1), 1),
    ):

        def table_step(cell, carry, src_ref=src_ref, base=base):
            tables(src_ref, base, cell)
            return carry

        lax.fori_loop(0, planes * plane, table_step, 0, unroll=2)
    pos_ref[wide] = jnp.full((3, n), AWAY, jnp.float32)

    diag_ref[0] = jnp.zeros((n, n), jnp.float32)
    diag_ref[1] = (
        lax.broadcasted_iota(jnp.int32, (n, n), 0) == lax.broadcasted_iota(jnp.int32, (n, n), 1)
    ).astype(jnp.float32)
    col_ref[...] = jnp.zeros_like(col_ref)
    acc_ref[...] = jnp.zeros_like(acc_ref)
    row_force_ref[...] = jnp.zeros_like(row_force_ref)
    lhs1_ref[...] = jnp.zeros_like(lhs1_ref)

    lane = lax.broadcasted_iota(jnp.int32, (1, n), 1)

    def own_step(cell, carry):
        for a in range(3):
            row = pos_ref[home_of(cell), a : a + 1, :]
            own_ref[cell, a] = lanes_to_sublanes(jnp.where(lane < count_of(cell), row, -AWAY))
        return carry

    lax.fori_loop(0, cells, own_step, 0)

    def where_of(index):
        entry = tiles_ref[index]
        return entry & 7, (entry >> 3) & 1, (entry >> 4) & 63, entry >> 10

    def far_rows(place):
        return [pos_ref[place, a : a + 1, :] for a in range(3)]

    def wide_table(table_ref, far):
        return jnp.concatenate([table_ref[far, m] for m in range(NB)], axis=1)

    def shape_tile(index, lhs_ref, after):
        cell, self_tile, _, place = where_of(index)
        first_rows = far_rows(place)
        marks = [after] * SHAPE_DEPTH
        for r in range(0, n, ROWS):
            at = pl.ds(r, ROWS)
            rows = behind(first_rows, marks[-SHAPE_DEPTH])
            d = [rows[a] - own_ref[cell, a, at, :] for a in range(3)]
            q = d[0] * d[0] + d[1] * d[1] + d[2] * d[2]
            q = jnp.minimum(jnp.maximum(q, diag_ref[self_tile, at, :]), 1.0)
            t = 1.0 - q
            u = t * t
            x = horner(COS, q)
            inverse = lax.rsqrt(q)
            waves = orders(x)
            for k, kept in enumerate((t, x, inverse, waves[2], waves[3])):
                geo_ref[index, k, at, :] = kept
            for m in range(NB):
                b = u * waves[m] if m else u
                w = b * inverse
                lhs_ref[m, at, :] = b.astype(jnp.bfloat16)
                for a in range(3):
                    lhs_ref[m, pl.ds((a + 1) * n + r, ROWS), :] = (w * d[a]).astype(jnp.bfloat16)
            marks.append(zeros_after(w))
        return marks[-1]

    def gather_tile(index, lhs_ref):
        cell, _, far, _ = where_of(index)

        def contract(rows, table_ref):
            lhs = jnp.concatenate([lhs_ref[m, rows, :] for m in range(NB)], axis=1)
            return lax.dot_general(
                lhs,
                wide_table(table_ref, far),
                (((1,), (1,)), ((), ())),
                preferred_element_type=jnp.float32,
            )

        acc_ref[cell, 0:n, :] += contract(pl.ds(0, n), s_ref)
        last = contract(pl.ds(n, 3 * n), v_ref)
        acc_ref[cell, n:, :] += last
        return zeros_after(last[3 * n - 8 :, :])

    lhs_refs = (lhs0_ref, lhs1_ref)

    def forward(group, carry):
        first = UNROLL * group
        gathered = [None] * LAG + [gather_tile(jnp.maximum(first - 1, 0), lhs1_ref)]
        after = None
        for k in range(UNROLL):
            if gathered[k] is not None:
                after = gathered[k] if after is None else after + gathered[k]
            after = shape_tile(first + k, lhs_refs[k % 2], after)
            if k < UNROLL - 1:
                gathered.append(gather_tile(first + k, lhs_refs[k % 2]))
        return carry

    lax.fori_loop(0, groups, forward, 0)
    gather_tile(UNROLL * groups - 1, lhs1_ref)

    def update(cell, carry):
        m0 = acc_ref[cell, 0:n, :]
        ma = [acc_ref[cell, (a + 1) * n : (a + 2) * n, :] for a in range(3)]
        own_feature = mid_ref[home_of(cell) - plane, 0:n, :].astype(jnp.float32).T
        z = own_feature + m0 + (ma[0] * ma[0] + ma[1] * ma[1] + ma[2] * ma[2])
        hidden = jnp.dot(
            z.astype(jnp.bfloat16), mix_ref[...], preferred_element_type=jnp.float32
        )
        sigmoid = 1.0 / (1.0 + jnp.exp(-hidden))
        weight = out_weight_ref[...]
        count = count_of(cell)
        per = (weight * hidden * sigmoid).T
        energy_ref[pl.ds(cell, 1), :] = jnp.where(
            lane < count, jnp.sum(per, axis=0, keepdims=True), 0.0
        )
        alive = lax.broadcasted_iota(jnp.int32, (n, n), 0) < count
        derivative = sigmoid * (1.0 + hidden * (1.0 - sigmoid))
        tangent = jnp.where(alive, weight * derivative, 0.0).astype(jnp.bfloat16)
        g = lax.dot_general(
            tangent, mix_ref[...], (((1,), (1,)), ((), ())), preferred_element_type=jnp.float32
        )
        grad_ref[cell, 0:n, :] = g.astype(jnp.bfloat16)
        for a in range(3):
            grad_ref[cell, (a + 1) * n : (a + 2) * n, :] = (2.0 * ma[a] * g).astype(jnp.bfloat16)
        return carry

    lax.fori_loop(0, cells, update, 0)

    def sense_tile(index, pull_ref, turn_ref):
        cell, _, far, _ = where_of(index)

        pull_ref[...] = jnp.dot(
            grad_ref[cell, 0:n, :], wide_table(s_ref, far), preferred_element_type=jnp.float32
        )
        turn_ref[...] = jnp.dot(
            grad_ref[cell, n:, :], wide_table(v_ref, far), preferred_element_type=jnp.float32
        )

    def force_tile(index, pull_ref, turn_ref, after):
        cell, _, far, place = where_of(index)
        first_rows = far_rows(place)
        marks = [after] * FORCE_DEPTH
        col = [jnp.zeros((8, n), jnp.float32) for _ in range(3)]
        for r in range(0, n, 8):
            at = pl.ds(r, 8)
            rows = behind(first_rows, marks[-FORCE_DEPTH])
            d = [rows[a] - own_ref[cell, a, at, :] for a in range(3)]
            t, x, inverse, c2, c3 = [geo_ref[index, k, at, :] for k in range(5)]
            u = t * t
            s2, s3 = 4.0 * x, 6.0 * c2 + 3.0

            def value(v):
                return (v[0] + x * v[1]) + (c2 * v[2] + c3 * v[3])

            def slope(v):
                return v[1] + (s2 * v[2] + s3 * v[3])

            pulls = [pull_ref[at, pl.ds(m * n, n)] for m in range(NB)]
            e1, e2 = value(pulls), slope(pulls)
            values, slopes = [], []
            for a in range(3):
                turns = [turn_ref[pl.ds(a * n + r, 8), pl.ds(m * n, n)] for m in range(NB)]
                values.append(value(turns))
                slopes.append(slope(turns))
            e3 = d[0] * values[0] + d[1] * values[1] + d[2] * values[2]
            e4 = d[0] * slopes[0] + d[1] * slopes[1] + d[2] * slopes[2]
            ui = u * inverse
            sine2 = jnp.maximum(1.0 - c2, 1e-12)
            bend = (HALF_ROOT_PI * 0.5) * (sine2 * lax.rsqrt(sine2))
            along = (
                (-4.0 * t) * (e1 + inverse * e3)
                + (ui * bend) * (e2 + inverse * e4)
                - (ui * (inverse * inverse)) * e3
            )
            for a in range(3):
                f = d[a] * along + ui * values[a]
                row_force_ref[cell, a, at, :] += f
                col[a] = col[a] + f
            marks.append(zeros_after(col[0]))
        for a in range(3):
            col_ref[far, a] += col[a]
        return marks[-1]

    sense_refs = ((pull0_ref, turn0_ref), (pull1_ref, turn1_ref))

    def backward(group, carry):
        first = UNROLL * group
        after = None
        for k in range(UNROLL):
            sense_tile(jnp.minimum(first + k + 1, length), *sense_refs[(k + 1) % 2])
            after = force_tile(first + k, *sense_refs[k % 2], after)
        return carry

    sense_tile(0, *sense_refs[0])
    lax.fori_loop(0, groups, backward, 0)

    def finish(cell, carry):
        for a in range(3):
            force_ref[cell, a : a + 1, :] = jnp.sum(
                row_force_ref[cell, a].T, axis=0, keepdims=True
            )
        return carry

    lax.fori_loop(0, cells, finish, 0)

    def reduce(e, carry):
        react_ref[e] = jnp.sum(col_ref[e], axis=1)
        return carry

    lax.fori_loop(0, plane * (cells_x + 2), reduce, 0)


def local(dims, mask, held, before, mid, after, scalar, vector, mix, out_weight):
    cells_x, cells_y, cells_z = dims
    cells = cells_x * cells_y * cells_z
    wide = (cells_x + 2) * (cells_y + 2) * (cells_z + 2)
    n = 128
    vmem = pl.BlockSpec(memory_space=pltpu.VMEM)
    smem = pl.BlockSpec(memory_space=pltpu.SMEM)
    f32, bf16 = jnp.float32, jnp.bfloat16
    return pl.pallas_call(
        functools.partial(kernel, dims),
        out_shape=(
            jax.ShapeDtypeStruct((cells, n), f32),
            jax.ShapeDtypeStruct((cells, 3, n), f32),
            jax.ShapeDtypeStruct((wide, 3, n), f32),
        ),
        in_specs=[smem, smem] + [vmem] * 7,
        out_specs=(vmem, vmem, vmem),
        scratch_shapes=[
            pltpu.SMEM((27 * cells + UNROLL,), jnp.int32),
            pltpu.VMEM((2 * NB, n, n), f32),
            pltpu.VMEM((wide + 1, 3, n), f32),
            pltpu.VMEM((wide, NB, n, n), bf16),
            pltpu.VMEM((wide, NB, n, n), bf16),
            pltpu.VMEM((cells, 3, n, n), f32),
            pltpu.VMEM((2, n, n), f32),
            pltpu.VMEM((27 * cells + UNROLL, 5, n, n), f32),
            pltpu.VMEM((NB, 4 * n, n), bf16),
            pltpu.VMEM((NB, 4 * n, n), bf16),
            pltpu.VMEM((cells, 4 * n, n), f32),
            pltpu.VMEM((cells, 4 * n, n), bf16),
            pltpu.VMEM((n, NB * n), f32),
            pltpu.VMEM((3 * n, NB * n), f32),
            pltpu.VMEM((n, NB * n), f32),
            pltpu.VMEM((3 * n, NB * n), f32),
            pltpu.VMEM((cells, 3, n, n), f32),
            pltpu.VMEM((wide, 3, 8, n), f32),
        ],
        compiler_params=pltpu.CompilerParams(vmem_limit_bytes=61 * 1024 * 1024,
        ),
        name="pair_kernel",
    )(mask, held, before, mid, after, scalar, vector, mix, out_weight.reshape(1, n))


def swap(axis, up_value, down_value):
    devices = lax.axis_size(axis)
    up = [(i, (i + 1) % devices) for i in range(devices)]
    down = [(j, i) for i, j in up]
    return lax.ppermute(up_value, axis, up), lax.ppermute(down_value, axis, down)


def widened(shard, axis, dim):
    length = shard.shape[dim]
    last = lax.slice_in_dim(shard, length - 1, length, axis=dim)
    leading = lax.slice_in_dim(shard, 0, 1, axis=dim)
    return swap(axis, last, leading)


def returned(wide, axis, dim):
    length = wide.shape[dim]
    high = lax.slice_in_dim(wide, length - 1, length, axis=dim)
    low = lax.slice_in_dim(wide, 0, 1, axis=dim)
    from_below, from_above = swap(axis, high, low)
    core = lax.slice_in_dim(wide, 1, length - 1, axis=dim)
    rest = length - 3

    def pad(piece, lo, hi):
        widths = [(0, 0)] * wide.ndim
        widths[dim] = (lo, hi)
        return jnp.pad(piece, widths)

    return core + pad(from_below, 0, rest) + pad(from_above, rest, 0)


def packed(positions, features, cell_count):
    n = positions.shape[-1]
    slots = jnp.arange(n, dtype=jnp.int32)
    rest = jnp.where(slots < cell_count[..., None, None], positions, AWAY)
    parts = []
    for _ in range(3):
        part = lax.reduce_precision(rest, 8, 7)
        parts.append(part)
        rest = rest - part
    spare = HEIGHT - n - 9
    parts.append(jnp.zeros(rest.shape[:3] + (spare, n), rest.dtype))
    rows = jnp.concatenate(parts, axis=3).astype(jnp.bfloat16)
    return jnp.concatenate([features, rows], axis=3)


def shards(
    positions, features, cell_count, pair_mask, scalar_radial, vector_radial, mix_weight, out_weight
):
    cells_x, cells_y, cells_z, _, n = positions.shape
    block = packed(positions, features, cell_count)
    for axis, dim in (("gz", 2), ("gy", 1)):
        below, above = widened(block, axis, dim)
        block = jnp.concatenate([below, block, above], axis=dim)
    before, after = widened(block, "gx", 0)
    flat = lambda v: v.reshape((-1,) + v.shape[3:])
    energy, force, react = local(
        (cells_x, cells_y, cells_z),
        pair_mask,
        cell_count,
        flat(before),
        flat(block),
        flat(after),
        scalar_radial,
        vector_radial,
        mix_weight,
        out_weight,
    )
    react = react.reshape(cells_x + 2, cells_y + 2, cells_z + 2, 3, n)
    for axis, dim in (("gx", 0), ("gy", 1), ("gz", 2)):
        react = returned(react, axis, dim)
    return (
        energy.reshape(cells_x, cells_y, cells_z, n),
        force.reshape(cells_x, cells_y, cells_z, 3, n) - react,
    )


def solution(mesh):
    return jax.shard_map(
        shards,
        mesh=mesh,
        in_specs=(
            P("gx", "gy", "gz", None, None),
            P("gx", "gy", "gz", None, None),
            P("gx", "gy", "gz"),
            P(None, "gx", "gy", "gz"),
            P(),
            P(),
            P(),
            P(),
        ),
        out_specs=(P("gx", "gy", "gz", None), P("gx", "gy", "gz", None, None)),
        check_vma=False,
    )
```
